32 devices in a mesh: tm: 2 (over x), space: 16 (over z, y, core).
Axes of the slice: x: 2, y: 2, z: 4, core: 2. Of those that a mesh axis runs over, the one named last changes fastest.
Arguments:
- frames: float32 [8, 256, 1024], P('tm', 'space'), may hold values from -6 to 6
- seeding: int32 [8, 16, 64], P('tm', 'space'), may hold values from 0 to 1, as said below
- lags: int32 [4], replicated, may hold values from 1 to 4, as said below
Outputs:
- ensemble: float32 [16, 64, 4, 1024], P('space', 'tm')
The draws below stay inside these ranges and needn't reach their ends.
Inputs may be any that keep to these rules, and one draw needn't show every extreme that they name: `lags`: a permutation of 1 to 4. `seeding`: flags are 0 or 1; in every row of window anchors at least one window is seeded in all frames.
All inputs are finite; a program needn't handle non-finite values.
Results may differ from the reference program's by a relative error of at most 0.0003.
Values sent between devices are 32-bit elements; how exact they have to be, the bound alone decides.
No kernel may reach another device: no remote copies, remote signals or barrier semaphores. Data moves between devices by JAX's collectives and lax.ppermute only.
A program may use at most 192 MiB of HBM per device.

```python
import jax
import jax.numpy as jnp
from jax import lax

FRAMES = 8
NLAG = 4
WIN = 64
STRIDE = 16
SPAN = 32
COLS = 1024
ROWS = 256
WROWS = 16
WCOLS = 64


def draw_seeding(key, part):
    row_ids = jnp.arange(WROWS, dtype=jnp.int32)
    distance = jnp.abs(2 * row_ids + 1 - 2 * (WROWS // 2))
    threshold = jnp.where(distance < WROWS // 4, 90, jnp.where(distance < WROWS // 2, 40, 10))
    rolls = jax.random.randint(key, (FRAMES, WROWS, WCOLS), 0, 100)
    seeded = (rolls < threshold[None, :, None]).astype(jnp.int32)
    chosen = jax.random.randint(jax.random.fold_in(key, 1), (WROWS,), 0, WCOLS)
    forced = (chosen[:, None] == jnp.arange(WCOLS, dtype=jnp.int32)[None, :]).astype(jnp.int32)
    return jnp.maximum(seeded, forced[None, :, :]).astype(jnp.int32)


def draw_lags(key, part):
    return (jax.random.permutation(key, NLAG) + 1).astype(jnp.int32)


def block_levels(stream_key, extent, split, low, high):
    level = 1.0
    for dim, blocks in split:
        heights = jax.random.uniform(jax.random.fold_in(jax.random.fold_in(stream_key, 6), dim), (blocks,), jnp.float32, low / len(split), high / len(split))
        level = level * jnp.repeat(jnp.exp(heights), extent[dim] // blocks).reshape((-1,) + (1,) * (len(extent) - 1 - dim))
    return level


def bell_draw(stream_key, dims, deviation, most, cuts=(), kind=jnp.bfloat16):
    values = jax.random.normal(stream_key, dims, jnp.float32) * deviation
    if len(cuts) > 0:
        values = block_levels(stream_key, dims, cuts, -0.22, 0.18) * values
    return jnp.clip(values, min=-most, max=most).astype(kind)


def setup_inputs(seed: int = 0) -> dict:
    seeds = jax.random.split(jax.random.key(seed), 4)
    return {
        "frames": bell_draw(seeds[0], (FRAMES, ROWS, COLS), 1.0, 6.0, ((0, 2), (1, 16)), jnp.float32),
        "seeding": draw_seeding(jax.random.fold_in(seeds[3], 71), 0),
        "lags": draw_lags(jax.random.fold_in(seeds[3], 71), 0),
    }


def reference(frames, seeding, lags):
    column_count = frames.shape[2]
    window_rows = frames.shape[1] // STRIDE
    window_cols = column_count // STRIDE
    extra_cols = WIN - STRIDE
    padded = jnp.pad(frames, ((0, 0), (0, extra_cols), (0, extra_cols)))
    centre = ((jnp.arange(SPAN) - SPAN // 2) % WIN).astype(jnp.int32)
    partner_index = ((jnp.arange(FRAMES)[None, :] + lags[:, None]) % FRAMES).astype(jnp.int32)
    pairs = seeding[None] * seeding[partner_index]
    counts = lax.optimization_barrier(jnp.sum(pairs, axis=1))
    column_index = (jnp.arange(window_cols)[:, None] * STRIDE + jnp.arange(WIN)[None, :]).astype(jnp.int32)

    def one_row(row_number):
        window_band = lax.dynamic_slice_in_dim(padded, row_number * STRIDE, WIN, 1)
        windows = jnp.transpose(window_band[:, :, column_index], (0, 2, 1, 3))
        window_mean = lax.optimization_barrier(jnp.mean(windows, axis=(2, 3), keepdims=True))
        centred = windows - window_mean
        normed = centred / jnp.sqrt(lax.optimization_barrier(jnp.mean(centred * centred, axis=(2, 3), keepdims=True)) + 1e-06)
        spectrum = jnp.fft.fft2(normed)
        outputs = []
        for number in range(NLAG):
            partner = spectrum[partner_index[number]]
            correlation = jnp.real(jnp.fft.ifft2(jnp.conj(spectrum) * partner))
            correlation = correlation[:, :, centre][:, :, :, centre] / WIN
            weight = lax.dynamic_index_in_dim(pairs[number], row_number, 1, keepdims=False).astype(jnp.float32)
            summed = lax.optimization_barrier(jnp.sum(weight[:, :, None, None] * correlation, axis=0))
            row_counts = lax.dynamic_index_in_dim(counts[number], row_number, 0, keepdims=False)
            divisor = jnp.maximum(row_counts, 1).astype(jnp.float32)
            outputs.append(summed.reshape(window_cols, SPAN * SPAN) / divisor[:, None])
        return jnp.stack(outputs, axis=1)
    return lax.map(one_row, jnp.arange(window_rows, dtype=jnp.int32))
```

```python
import functools
import math

import jax
import jax.numpy as jnp
import numpy as np
from jax import lax
from jax.experimental import pallas as pl
from jax.experimental.pallas import tpu as pltpu
from jax.sharding import PartitionSpec as P

WIN = 64
STRIDE = 16
SPAN = 32
HALF = WIN // 2
GROUP = 8
LANES = 128
BLOCK = GROUP * STRIDE
REACH = 2 * BLOCK
EXTRA = WIN - STRIDE


def split_table(table):
    table = np.asarray(table, np.float32)
    high = jnp.asarray(table).astype(jnp.bfloat16)
    low = (jnp.asarray(table) - high.astype(jnp.float32)).astype(jnp.bfloat16)
    return high, low


def turn(product):
    return 2.0 * math.pi / WIN * np.asarray(np.mod(product, WIN), np.float64)


def forward_rows():
    place = np.arange(WIN)
    u = np.arange(HALF)
    cos_rows = np.cos(turn(np.outer(u, place)))
    sin_rows = -np.sin(turn(np.outer(u, place)))
    sin_rows[0] = np.cos(turn(HALF * place))
    return np.concatenate([cos_rows, sin_rows], axis=0)


def forward_cols():
    rows = forward_rows()
    table = np.zeros((REACH, 2, GROUP, HALF))
    for g in range(GROUP):
        table[g * STRIDE : g * STRIDE + WIN, 0, g] = rows[:HALF].T
        table[g * STRIDE : g * STRIDE + WIN, 1, g] = rows[HALF:].T
    return table.reshape(REACH, 2 * GROUP * HALF)


def inverse_parts():
    place = np.arange(SPAN) - SPAN // 2
    u = np.arange(HALF)
    cos_part = np.cos(turn(np.outer(place, u)))
    sin_part = np.sin(turn(np.outer(place, u)))
    sin_part[:, 0] = np.cos(turn(HALF * place))
    return cos_part, sin_part


def inverse_rows(lag_count):
    cos_part, sin_part = inverse_parts()
    sin_part = -sin_part
    sin_part[:, 0] = -sin_part[:, 0]
    both = np.concatenate([cos_part, sin_part], axis=1)
    table = np.zeros((SPAN // 8, 4, 2, lag_count, lag_count, 2 * HALF))
    for block in range(SPAN // 8):
        for j in range(4):
            for side in range(2):
                for k in range(lag_count):
                    table[block, j, side, k, k] = both[block * 8 + side * 4 + j]
    return table.reshape(SPAN * lag_count, lag_count * 2 * HALF)


def inverse_cols():
    cos_part, sin_part = inverse_parts()
    table = np.zeros((2, GROUP, HALF, GROUP, SPAN))
    for g in range(GROUP):
        table[0, g, :, g] = cos_part.T
        table[1, g, :, g] = sin_part.T
    scale = 2.0 / (WIN * WIN * WIN)
    return table.reshape(2 * GROUP * HALF, GROUP * SPAN) * scale


def halves(value):
    high = value.astype(jnp.bfloat16)
    low = (value - high.astype(jnp.float32)).astype(jnp.bfloat16)
    return high, low


def mul(a, b):
    return jnp.dot(a, b, preferred_element_type=jnp.float32)


def kernel(
    layout, frame_count, lag_count, block_count,
    lags_ref, flags_ref, ty_ref, txh_ref, txl_ref, iyh_ref, iyl_ref, ixh_ref, ixl_ref, *rest,
):
    piece_count = len(rest) - 4
    pieces, out_ref = rest[:piece_count], rest[piece_count]
    spec_ref, corner_ref, y_ref = rest[piece_count + 1 :]
    wide = GROUP * HALF

    lane = lax.broadcasted_iota(jnp.int32, (8, wide), 1)
    sub = lax.broadcasted_iota(jnp.int32, (8, wide), 0)
    slot0 = lane % HALF == 0
    row0 = sub == 0
    corner = jnp.logical_and(slot0, row0)

    gather_lane = lax.broadcasted_iota(jnp.int32, (wide, wide), 1) // HALF
    gather_row = lax.broadcasted_iota(jnp.int32, (wide, wide), 0) // HALF
    same = (gather_lane == gather_row).astype(jnp.float32).astype(jnp.bfloat16)

    def block_step(i, carry):
        column = pl.multiple_of(i * BLOCK, BLOCK)
        sums = []
        for f in range(frame_count):
            parts = [pieces[p][q, :, pl.ds(column, REACH)] for p, q in layout[f]]
            image = jnp.concatenate(parts, axis=0)
            high, low = halves(image)
            tall = jnp.concatenate([high, low, high], axis=0)
            middle = mul(ty_ref[...], tall)
            high, low = halves(middle)
            spec = mul(high, txh_ref[...]) + mul(low, txh_ref[...]) + mul(high, txl_ref[...])
            total = None
            for t in range(HALF // 8):
                a = spec[8 * t : 8 * t + 8, :wide]
                b = spec[8 * t : 8 * t + 8, wide:]
                c = spec[HALF + 8 * t : HALF + 8 * t + 8, :wide]
                d = spec[HALF + 8 * t : HALF + 8 * t + 8, wide:]
                p0 = jnp.where(slot0, a, a - d)
                q0 = jnp.where(slot0, c, c + b)
                p1 = jnp.where(slot0, b, a + d)
                q1 = jnp.where(slot0, d, c - b)
                if t == 0:
                    p0 = jnp.where(corner, 0.0, jnp.where(row0, a, p0))
                    q0 = jnp.where(row0, b, q0)
                    p1 = jnp.where(row0, c, p1)
                    q1 = jnp.where(corner, 0.0, jnp.where(row0, d, q1))
                    last = jnp.where(corner, d, 0.0)
                    corner_ref[f] = last
                    square = p0 * p0 + q0 * q0 + p1 * p1 + q1 * q1 + last * last
                    total = jnp.where(corner, 0.5 * square, square)
                else:
                    total = total + (p0 * p0 + q0 * q0 + p1 * p1 + q1 * q1)
                spec_ref[f, 0, 8 * t : 8 * t + 8, :] = p0
                spec_ref[f, 1, 8 * t : 8 * t + 8, :] = q0
                spec_ref[f, 2, 8 * t : 8 * t + 8, :] = p1
                spec_ref[f, 3, 8 * t : 8 * t + 8, :] = q1
            sums.append(jnp.sum(total, axis=0, keepdims=True))
        power = jnp.concatenate(sums, axis=0)
        high, low = halves(power)
        power = mul(high, same) + mul(low, same)
        variance = power * (2.0 / (WIN * WIN * WIN * WIN))

        flag_row = lax.broadcasted_iota(jnp.int32, (LANES, wide), 0)
        flag_lane = lax.broadcasted_iota(jnp.int32, (LANES, wide), 1)
        pick = (flag_row == i * GROUP + flag_lane // HALF).astype(jnp.float32).astype(jnp.bfloat16)
        flags = mul(flags_ref[...].astype(jnp.bfloat16), pick)
        gain = flags / jnp.sqrt(variance + 1e-06)

        counts = []
        for number in range(lag_count):
            ahead = jnp.concatenate([flags[number + 1 :], flags[: number + 1]], axis=0)
            counts.append(jnp.sum(flags * ahead, axis=0, keepdims=True))
        scale_rows = []
        for k in range(lag_count):
            count = counts[0]
            for number in range(1, lag_count):
                count = jnp.where(lags_ref[k] == number + 1, counts[number], count)
            scale_rows.append(1.0 / jnp.maximum(count, 1.0))
        scale = jnp.concatenate(scale_rows + scale_rows, axis=0)

        places = []
        for number in range(lag_count):
            place = jnp.int32(0)
            for k in range(lag_count):
                place = jnp.where(lags_ref[k] == number + 1, k, place)
            places.append(place)

        for l in range(wide // LANES):
            at = slice(l * LANES, (l + 1) * LANES)
            gains = [jnp.broadcast_to(gain[f : f + 1, at], (8, LANES)) for f in range(frame_count)]
            m0 = slot0[:, at]
            r0 = row0[:, at]
            co = corner[:, at]
            for t in range(HALF // 8):
                rows = slice(8 * t, 8 * t + 8)
                results = []
                for side in range(2):
                    ps = [spec_ref[f, 2 * side, rows, at] * gains[f] for f in range(frame_count)]
                    qs = [spec_ref[f, 2 * side + 1, rows, at] * gains[f] for f in range(frame_count)]
                    sums_of_lags = []
                    for number in range(lag_count):
                        lag = number + 1
                        real = None
                        imag = None
                        twice = 2 * lag == frame_count
                        for f in range(frame_count // 2 if twice else frame_count):
                            g = (f + lag) % frame_count
                            re = ps[f] * ps[g] + qs[f] * qs[g]
                            real = re if real is None else real + re
                            if not twice:
                                im = ps[f] * qs[g] - qs[f] * ps[g]
                                imag = im if imag is None else imag + im
                        if twice:
                            real = real + real
                            imag = jnp.zeros_like(real)
                        sums_of_lags.append((real, imag))
                    results.append(sums_of_lags)
                if t == 0:
                    ends = [corner_ref[f, :, at] * gains[f] for f in range(frame_count)]
                for number in range(lag_count):
                    p0, q0 = results[0][number]
                    p1, q1 = results[1][number]
                    ya = jnp.where(m0, p0, p0 + p1)
                    yb = jnp.where(m0, p1, q1 - q0)
                    yc = jnp.where(m0, q0, q0 + q1)
                    yd = jnp.where(m0, q1, p0 - p1)
                    if t == 0:
                        last = ends[0] * ends[number + 1]
                        for f in range(1, frame_count):
                            last = last + ends[f] * ends[(f + number + 1) % frame_count]
                        ya = jnp.where(co, 0.0, jnp.where(r0, p0, ya))
                        yb = jnp.where(co, 0.5 * p0, jnp.where(r0, -q0, yb))
                        yc = jnp.where(co, 0.5 * p1, jnp.where(r0, p1, yc))
                        yd = jnp.where(co, 0.5 * last, jnp.where(r0, -q1, yd))
                    start = places[number] * (2 * HALF)
                    top = pl.ds(pl.multiple_of(start + 8 * t, 8), 8)
                    bottom = pl.ds(pl.multiple_of(start + HALF + 8 * t, 8), 8)
                    y_ref[top, l * LANES : (l + 1) * LANES] = ya
                    y_ref[top, wide + l * LANES : wide + (l + 1) * LANES] = yb
                    y_ref[bottom, l * LANES : (l + 1) * LANES] = yc
                    y_ref[bottom, wide + l * LANES : wide + (l + 1) * LANES] = yd

        high, low = halves(y_ref[...])
        part = mul(iyh_ref[...], high) + mul(iyh_ref[...], low) + mul(iyl_ref[...], high)
        high, low = halves(part)
        final = mul(high, ixh_ref[...]) + mul(low, ixh_ref[...]) + mul(high, ixl_ref[...])

        lane128 = lax.broadcasted_iota(jnp.int32, (8, LANES), 1)
        first_half = lane128 < LANES // 2
        even = (lane128 // SPAN) % 2 == 0
        for run in range(SPAN // 8):
            for l in range(GROUP * SPAN // LANES):
                v = []
                for j in range(4):
                    r = (run * 4 + j) * 8
                    v.append(final[r : r + 8, l * LANES : (l + 1) * LANES] * scale[:, l * LANES : (l + 1) * LANES])
                for j in range(2):
                    x, y = v[j], v[j + 2]
                    v[j] = jnp.where(first_half, x, pltpu.roll(y, LANES // 2, 1))
                    v[j + 2] = jnp.where(first_half, pltpu.roll(x, LANES // 2, 1), y)
                for j in (0, 2):
                    x, y = v[j], v[j + 1]
                    v[j] = jnp.where(even, x, pltpu.roll(y, SPAN, 1))
                    v[j + 1] = jnp.where(even, pltpu.roll(x, LANES - SPAN, 1), y)
                for j in range(4):
                    window = i * GROUP + 4 * l + j
                    for side in range(2):
                        first = (2 * run + side) * LANES
                        out_ref[0, window, :, first : first + LANES] = v[j][4 * side : 4 * side + 4]
        return carry

    lax.fori_loop(0, block_count, block_step, 0)


def correlate(lags, flags, layout, pieces, window_cols):
    frame_count = len(layout)
    lag_count = lags.shape[0]
    wide = GROUP * HALF
    ty_high, ty_low = split_table(forward_rows())
    ty = jnp.concatenate([ty_high, ty_high, ty_low], axis=1)
    txh, txl = split_table(forward_cols())
    iyh, iyl = split_table(inverse_rows(lag_count))
    ixh, ixl = split_table(inverse_cols())
    vmem = pl.BlockSpec(memory_space=pltpu.VMEM)
    body = functools.partial(kernel, layout, frame_count, lag_count, window_cols // GROUP)
    return pl.pallas_call(
        body,
        out_shape=jax.ShapeDtypeStruct((1, window_cols, lag_count, SPAN * SPAN), jnp.float32),
        in_specs=[pl.BlockSpec(memory_space=pltpu.SMEM)] + [vmem] * (8 + len(pieces)),
        out_specs=vmem,
        scratch_shapes=[
            pltpu.VMEM((frame_count, 4, HALF, wide), jnp.float32),
            pltpu.VMEM((frame_count, 8, wide), jnp.float32),
            pltpu.VMEM((lag_count * 2 * HALF, 2 * wide), jnp.float32),
        ],
    )(lags, flags, ty, txh, txl, iyh, iyl, ixh, ixl, *pieces)


def per_device(frames, seeding, lags):
    frame_count, band_rows, columns = frames.shape
    time_devices = lax.axis_size("tm")
    space_devices = lax.axis_size("space")
    block_cols = columns // time_devices
    window_cols = block_cols // STRIDE
    width = -(-(block_cols + EXTRA + window_cols) // LANES) * LANES
    padded = jnp.pad(frames, ((0, 0), (0, 0), (0, width)))
    flags = seeding[:, 0, :].astype(jnp.float32)
    me = lax.axis_index("tm")
    bands = [lax.dynamic_slice_in_dim(padded, me * block_cols, width, 2)]
    marks = [lax.dynamic_slice_in_dim(flags, me * window_cols, window_cols, 1)]
    for k in range(1, time_devices):
        route = [((i + k) % time_devices, i) for i in range(time_devices)]
        target = (me + time_devices - k) % time_devices
        block = lax.dynamic_slice_in_dim(padded, target * block_cols, width, 2)
        mark = lax.dynamic_slice_in_dim(flags, target * window_cols, window_cols, 1)
        bands.append(lax.ppermute(block, "tm", route))
        marks.append(lax.ppermute(mark, "tm", route))
    own = jnp.concatenate(bands, axis=0)
    marks = jnp.concatenate(marks, axis=0)
    marks = jnp.pad(marks, ((0, 0), (0, LANES - window_cols)))
    pieces = [own]
    for shift in range(1, WIN // band_rows):
        route = [(i + shift, i) for i in range(space_devices - shift)]
        pieces.append(lax.ppermute(own, "space", route))
    layout = [[(p, f) for p in range(len(pieces))] for f in range(own.shape[0])]
    return correlate(lags, marks, layout, pieces, window_cols)


def solution(mesh):
    return jax.shard_map(
        per_device,
        mesh=mesh,
        in_specs=(P("tm", "space", None), P("tm", "space", None), P()),
        out_specs=P("space", "tm", None, None),
        check_vma=False,
    )
```

```python
import functools
import math

import jax
import jax.numpy as jnp
import numpy as np
from jax import lax
from jax.experimental import pallas as pl
from jax.experimental.pallas import tpu as pltpu
from jax.sharding import PartitionSpec as P

WIN = 64
STRIDE = 16
SPAN = 32
HALF = WIN // 2
GROUP = 8
LANES = 128
BLOCK = GROUP * STRIDE
REACH = 2 * BLOCK
EXTRA = WIN - STRIDE
PARTS = 1


def split_table(table):
    table = np.asarray(table, np.float32)
    high = jnp.asarray(table).astype(jnp.bfloat16)
    low = (jnp.asarray(table) - high.astype(jnp.float32)).astype(jnp.bfloat16)
    return high, low


def turn(product):
    return 2.0 * math.pi / WIN * np.asarray(np.mod(product, WIN), np.float64)


def forward_rows():
    place = np.arange(WIN)
    u = np.arange(HALF)
    cos_rows = np.cos(turn(np.outer(u, place)))
    sin_rows = -np.sin(turn(np.outer(u, place)))
    sin_rows[0] = np.cos(turn(HALF * place))
    return np.concatenate([cos_rows, sin_rows], axis=0)


def forward_cols():
    rows = forward_rows()
    table = np.zeros((REACH, 2, GROUP, HALF))
    for g in range(GROUP):
        table[g * STRIDE : g * STRIDE + WIN, 0, g] = rows[:HALF].T
        table[g * STRIDE : g * STRIDE + WIN, 1, g] = rows[HALF:].T
    return table.reshape(REACH, 2 * GROUP * HALF)


def inverse_parts():
    place = np.arange(SPAN) - SPAN // 2
    u = np.arange(HALF)
    cos_part = np.cos(turn(np.outer(place, u)))
    sin_part = np.sin(turn(np.outer(place, u)))
    sin_part[:, 0] = np.cos(turn(HALF * place))
    return cos_part, sin_part


def inverse_rows(lag_count):
    cos_part, sin_part = inverse_parts()
    sin_part = -sin_part
    sin_part[:, 0] = -sin_part[:, 0]
    both = np.concatenate([cos_part, sin_part], axis=1)
    table = both.reshape(SPAN // 8, 2, 4, 1, 1, 2 * HALF).transpose(0, 2, 1, 3, 4, 5)
    table = np.broadcast_to(table, (SPAN // 8, 4, 2, lag_count, lag_count, 2 * HALF))
    return table.reshape(SPAN * lag_count, lag_count * 2 * HALF)


def inverse_cols():
    cos_part, sin_part = inverse_parts()
    table = np.zeros((2, GROUP, HALF, GROUP, SPAN))
    for g in range(GROUP):
        table[0, g, :, g] = cos_part.T
        table[1, g, :, g] = sin_part.T
    scale = 2.0 / (WIN * WIN * WIN)
    return table.reshape(2 * GROUP * HALF, GROUP * SPAN) * scale


def halves(value):
    high = value.astype(jnp.bfloat16)
    low = (value - high.astype(jnp.float32)).astype(jnp.bfloat16)
    return high, low


def mul(a, b):
    return jnp.dot(a, b, preferred_element_type=jnp.float32)


def cross_direct(ps, qs, lag_count):
    frame_count = len(ps)
    results = []
    for lag in range(1, lag_count + 1):
        real = imag = None
        for f in range(frame_count):
            g = (f + lag) % frame_count
            re = ps[f] * ps[g] + qs[f] * qs[g]
            im = ps[f] * qs[g] - qs[f] * ps[g]
            real = re if real is None else real + re
            imag = im if imag is None else imag + im
        results.append((real * frame_count, imag * frame_count))
    return results


def cross_eight(ps, qs):
    root = math.sqrt(0.5)
    sr = [ps[t] + ps[t + 4] for t in range(4)]
    si = [qs[t] + qs[t + 4] for t in range(4)]
    dr = [ps[t] - ps[t + 4] for t in range(4)]
    di = [qs[t] - qs[t + 4] for t in range(4)]
    e0r, e0i, e1r, e1i = sr[0] + sr[2], si[0] + si[2], sr[0] - sr[2], si[0] - si[2]
    o0r, o0i, o1r, o1i = sr[1] + sr[3], si[1] + si[3], sr[1] - sr[3], si[1] - si[3]

    def power(re, im):
        return re * re + im * im

    p0 = power(e0r + o0r, e0i + o0i)
    p4 = power(e0r - o0r, e0i - o0i)
    p2 = power(e1r + o1i, e1i - o1r)
    p6 = power(e1r - o1i, e1i + o1r)
    gpr, gpi, gmr, gmi = dr[0] + di[2], di[0] - dr[2], dr[0] - di[2], di[0] + dr[2]
    ar, ai, br, bi = dr[1] - dr[3], di[1] - di[3], dr[1] + dr[3], di[1] + di[3]
    hpr, hpi = root * (ar + bi), root * (ai - br)
    hmr, hmi = root * (bi - ar), root * (br + ai)
    p1 = power(gpr + hpr, gpi + hpi)
    p5 = power(gpr - hpr, gpi - hpi)
    p3 = power(gmr + hmr, gmi - hmi)
    p7 = power(gmr - hmr, gmi + hmi)
    a, b, c, d = p0 + p4, p0 - p4, p2 + p6, p2 - p6
    e, f, g, h = p1 + p5, p1 - p5, p3 + p7, p3 - p7
    less, more = root * (f - h), root * (f + h)
    return [
        (b + less, d + more),
        (a - c, e - g),
        (b - less, more - d),
        ((a + c) - (e + g), None),
    ]


def kernel(
    layout, frame_count, lag_count, block_count,
    lags_ref, flags_ref, ty_ref, txh_ref, txl_ref, iyh_ref, iyl_ref, ixh_ref, ixl_ref, *rest,
):
    piece_count = len(rest) - 11
    pieces, out_ref = rest[:piece_count], rest[piece_count]
    high_ref, low_ref, energy_ref, spec_ref, gain_ref, y_ref = rest[piece_count + 1 : piece_count + 7]
    part_ref, final_ref, pickh_ref, pickl_ref = rest[piece_count + 7 :]
    wide = GROUP * HALF
    rows_per = 2 * HALF
    width = pieces[0].shape[-1]

    lane = lax.broadcasted_iota(jnp.int32, (8, LANES), 1)
    sub = lax.broadcasted_iota(jnp.int32, (8, LANES), 0)
    m0 = lane % HALF == 0
    r0 = sub == 0
    co = jnp.logical_and(m0, r0)
    first_half = lane < LANES // 2
    even = (lane // SPAN) % 2 == 0
    slot0 = lax.broadcasted_iota(jnp.int32, (frame_count, wide), 1) % HALF == 0

    column = lax.broadcasted_iota(jnp.int32, (REACH, wide), 0)
    owner = lax.broadcasted_iota(jnp.int32, (REACH, wide), 1) // HALF
    inside = jnp.logical_and(column >= owner * STRIDE, column < owner * STRIDE + WIN)
    band = inside.astype(jnp.float32).astype(jnp.bfloat16)
    same = (column // HALF == owner).astype(jnp.float32).astype(jnp.bfloat16)

    wide_row0 = lax.broadcasted_iota(jnp.int32, (8, width), 0) == 0
    for f in range(frame_count):
        image = jnp.concatenate([pieces[p][q] for p, q in layout[f]], axis=0)
        high, low = halves(image)
        middle = mul(ty_ref[...], jnp.concatenate([high, low, high], axis=0))
        high, low = halves(middle)
        high_ref[f * rows_per : (f + 1) * rows_per, :] = high
        low_ref[f * rows_per : (f + 1) * rows_per, :] = low
        total = None
        for t in range(rows_per // 8):
            value = middle[8 * t : 8 * t + 8]
            square = value * value
            if t == 0:
                square = jnp.where(wide_row0, 0.0, square)
            if t == HALF // 8:
                square = jnp.where(wide_row0, 0.5 * square, square)
            total = square if total is None else total + square
        energy_ref[f : f + 1, :] = jnp.sum(total, axis=0, keepdims=True)

    chosen = lax.broadcasted_iota(jnp.int32, iyh_ref.shape, 0) % lag_count
    wanted = jnp.zeros(iyh_ref.shape, jnp.int32)
    for k in range(lag_count):
        wanted = jnp.where(chosen == k, lags_ref[k], wanted)
    block_of = lax.broadcasted_iota(jnp.int32, iyh_ref.shape, 1) // rows_per + 1
    keep = wanted == block_of
    pickh_ref[...] = jnp.where(keep, iyh_ref[...].astype(jnp.float32), 0.0).astype(jnp.bfloat16)
    pickl_ref[...] = jnp.where(keep, iyl_ref[...].astype(jnp.float32), 0.0).astype(jnp.bfloat16)

    scales = {}

    def forward_unit(i, n, part, parts):
        columns = slice(i * BLOCK, i * BLOCK + REACH)
        count = frame_count * rows_per // parts
        rows = slice(part * count, (part + 1) * count)
        at = slice(n * wide, (n + 1) * wide)
        spec_ref[i, rows, at] = (
            mul(high_ref[rows, columns], txh_ref[:, at])
            + mul(low_ref[rows, columns], txh_ref[:, at])
            + mul(high_ref[rows, columns], txl_ref[:, at])
        )

    def gain_unit(i):
        columns = slice(i * BLOCK, i * BLOCK + REACH)
        zero = jnp.concatenate(
            [spec_ref[i, f * rows_per : f * rows_per + 1, :] for f in range(frame_count)], axis=0
        )
        zero_re, zero_im = zero[:, :wide], zero[:, wide:]
        line = jnp.where(slot0, 0.5 * zero_im * zero_im, zero_re * zero_re + zero_im * zero_im)
        high, low = halves(line)
        line = mul(high, same) + mul(low, same)
        high, low = halves(energy_ref[:, columns])
        rest_of = mul(high, band) + mul(low, band)
        variance = rest_of * (2.0 * WIN / WIN**4) + line * (2.0 / WIN**4)

        flag_row = lax.broadcasted_iota(jnp.int32, (LANES, wide), 0)
        flag_lane = lax.broadcasted_iota(jnp.int32, (LANES, wide), 1)
        pick = (flag_row == i * GROUP + flag_lane // HALF).astype(jnp.float32).astype(jnp.bfloat16)
        flags = mul(flags_ref[...].astype(jnp.bfloat16), pick)
        gain_ref[i] = flags / jnp.sqrt(variance + 1e-06)

        counts = []
        for number in range(lag_count):
            ahead = jnp.concatenate([flags[number + 1 :], flags[: number + 1]], axis=0)
            counts.append(jnp.sum(flags * ahead, axis=0, keepdims=True))
        scale_rows = []
        for k in range(lag_count):
            count = counts[0]
            for number in range(1, lag_count):
                count = jnp.where(lags_ref[k] == number + 1, counts[number], count)
            scale_rows.append(1.0 / jnp.maximum(count, 1.0))
        scales[i] = jnp.concatenate(scale_rows * (8 // lag_count), axis=0)

    if frame_count == 8 and lag_count == 4:
        cross = cross_eight
    else:
        cross = functools.partial(cross_direct, lag_count=lag_count)

    def cross_unit(i, l, t):
        at = slice(l * LANES, (l + 1) * LANES)
        at_im = slice(wide + l * LANES, wide + (l + 1) * LANES)
        p0s, q0s, p1s, q1s, ends = [], [], [], [], []
        for f in range(frame_count):
            gain = jnp.broadcast_to(gain_ref[i, f : f + 1, at], (8, LANES))
            upper = slice(f * rows_per + 8 * t, f * rows_per + 8 * t + 8)
            lower = slice(f * rows_per + HALF + 8 * t, f * rows_per + HALF + 8 * t + 8)
            a = spec_ref[i, upper, at] * gain
            b = spec_ref[i, upper, at_im] * gain
            c = spec_ref[i, lower, at] * gain
            d = spec_ref[i, lower, at_im] * gain
            p0 = a - jnp.where(m0, 0.0, d)
            q0 = c + jnp.where(m0, 0.0, b)
            p1 = jnp.where(m0, b, a + d)
            q1 = jnp.where(m0, d, c - b)
            if t == 0:
                p0 = jnp.where(co, 0.0, jnp.where(r0, a, p0))
                q0 = jnp.where(r0, b, q0)
                p1 = jnp.where(r0, c, p1)
                q1 = jnp.where(co, 0.0, jnp.where(r0, d, q1))
                ends.append(jnp.where(co, d, 0.0))
            p0s.append(p0)
            q0s.append(q0)
            p1s.append(p1)
            q1s.append(q1)
        results0 = cross(p0s, q0s)
        results1 = cross(p1s, q1s)
        for number in range(lag_count):
            p0, q0 = results0[number]
            p1, q1 = results1[number]
            if q0 is None:
                ya = jnp.where(m0, p0, p0 + p1)
                yb = jnp.where(m0, p1, 0.0)
                yc = jnp.zeros_like(p0)
                yd = jnp.where(m0, 0.0, p0 - p1)
                q0 = q1 = yc
            else:
                ya = jnp.where(m0, p0, p0 + p1)
                yb = jnp.where(m0, p1, q1 - q0)
                yc = jnp.where(m0, q0, q0 + q1)
                yd = jnp.where(m0, q1, p0 - p1)
            if t == 0:
                last = ends[0] * ends[number + 1]
                for f in range(1, frame_count):
                    last = last + ends[f] * ends[(f + number + 1) % frame_count]
                ya = jnp.where(co, 0.0, jnp.where(r0, p0, ya))
                yb = jnp.where(co, 0.5 * p0, jnp.where(r0, -q0, yb))
                yc = jnp.where(co, 0.5 * p1, jnp.where(r0, p1, yc))
                yd = jnp.where(co, (0.5 * frame_count) * last, jnp.where(r0, -q1, yd))
            top = slice(number * rows_per + 8 * t, number * rows_per + 8 * t + 8)
            bottom = slice(number * rows_per + HALF + 8 * t, number * rows_per + HALF + 8 * t + 8)
            y_ref[i, top, at] = ya
            y_ref[i, top, at_im] = yb
            y_ref[i, bottom, at] = yc
            y_ref[i, bottom, at_im] = yd

    def inverse_unit(i, step):
        if step < 2:
            at = slice(step * wide, (step + 1) * wide)
            high, low = halves(y_ref[i, :, at])
            part_ref[i, :, at] = (
                mul(pickh_ref[...], high) + mul(pickh_ref[...], low) + mul(pickl_ref[...], high)
            )
        elif step == 2:
            high, low = halves(part_ref[i])
            final_ref[i] = mul(high, ixh_ref[...]) + mul(low, ixh_ref[...]) + mul(high, ixl_ref[...])
        else:
            scale = scales[i]
            for run in range(SPAN // 8):
                for l in range(GROUP * SPAN // LANES):
                    at = slice(l * LANES, (l + 1) * LANES)
                    v = []
                    for j in range(4):
                        r = (run * 4 + j) * 8
                        v.append(final_ref[i, r : r + 8, at] * scale[:, at])
                    for j in range(2):
                        x, y = v[j], v[j + 2]
                        v[j] = jnp.where(first_half, x, pltpu.roll(y, LANES // 2, 1))
                        v[j + 2] = jnp.where(first_half, pltpu.roll(x, LANES // 2, 1), y)
                    for j in (0, 2):
                        x, y = v[j], v[j + 1]
                        v[j] = jnp.where(even, x, pltpu.roll(y, SPAN, 1))
                        v[j + 1] = jnp.where(even, pltpu.roll(x, LANES - SPAN, 1), y)
                    for j in range(4):
                        window = i * GROUP + 4 * l + j
                        for side in range(2):
                            first = (2 * run + side) * LANES
                            out_ref[0, window, :, first : first + LANES] = v[j][4 * side : 4 * side + 4]

    spots = [(l, t) for l in range(wide // LANES) for t in range(HALF // 8)]
    for n in range(2):
        for part in range(PARTS):
            forward_unit(0, n, part, PARTS)
    gain_unit(0)
    for i in range(block_count + 1):
        queue = []
        if i > 0:
            queue += [functools.partial(inverse_unit, i - 1, step) for step in range(4)]
        if i + 1 < block_count:
            ahead = [
                functools.partial(forward_unit, i + 1, n, part, PARTS)
                for n in range(2)
                for part in range(PARTS)
            ]
            merged = []
            while queue or ahead:
                merged += ahead[:1] + queue[:1]
                queue, ahead = queue[1:], ahead[1:]
            queue = merged + [functools.partial(gain_unit, i + 1)]
        if i < block_count:
            for number, (l, t) in enumerate(spots):
                take = len(queue) * (number + 1) // len(spots) - len(queue) * number // len(spots)
                done = len(queue) * number // len(spots)
                for unit in queue[done : done + take]:
                    unit()
                cross_unit(i, l, t)
        else:
            for unit in queue:
                unit()


def correlate(lags, flags, layout, pieces, window_cols):
    frame_count = len(layout)
    lag_count = lags.shape[0]
    wide = GROUP * HALF
    width = pieces[0].shape[-1]
    block_count = window_cols // GROUP
    ty_high, ty_low = split_table(forward_rows())
    ty = jnp.concatenate([ty_high, ty_high, ty_low], axis=1)
    txh, txl = split_table(forward_cols())
    iyh, iyl = split_table(inverse_rows(lag_count))
    ixh, ixl = split_table(inverse_cols() / frame_count)
    vmem = pl.BlockSpec(memory_space=pltpu.VMEM)
    body = functools.partial(kernel, layout, frame_count, lag_count, block_count)
    return pl.pallas_call(
        body,
        out_shape=jax.ShapeDtypeStruct((1, window_cols, lag_count, SPAN * SPAN), jnp.float32),
        in_specs=[pl.BlockSpec(memory_space=pltpu.SMEM)] + [vmem] * (8 + len(pieces)),
        out_specs=vmem,
        scratch_shapes=[
            pltpu.VMEM((frame_count * 2 * HALF, width), jnp.bfloat16),
            pltpu.VMEM((frame_count * 2 * HALF, width), jnp.bfloat16),
            pltpu.VMEM((frame_count, width), jnp.float32),
            pltpu.VMEM((block_count, frame_count * 2 * HALF, 2 * wide), jnp.float32),
            pltpu.VMEM((block_count, frame_count, wide), jnp.float32),
            pltpu.VMEM((block_count, lag_count * 2 * HALF, 2 * wide), jnp.float32),
            pltpu.VMEM((block_count, lag_count * SPAN, 2 * wide), jnp.float32),
            pltpu.VMEM((block_count, lag_count * SPAN, GROUP * SPAN), jnp.float32),
            pltpu.VMEM(iyh.shape, jnp.bfloat16),
            pltpu.VMEM(iyl.shape, jnp.bfloat16),
        ],
    )(lags, flags, ty, txh, txl, iyh, iyl, ixh, ixl, *pieces)


def per_device(frames, seeding, lags):
    frame_count, band_rows, columns = frames.shape
    time_devices = lax.axis_size("tm")
    space_devices = lax.axis_size("space")
    block_cols = columns // time_devices
    window_cols = block_cols // STRIDE
    width = -(-(block_cols + EXTRA + window_cols) // LANES) * LANES
    padded = jnp.pad(frames, ((0, 0), (0, 0), (0, width)))
    flags = seeding[:, 0, :].astype(jnp.float32)
    me = lax.axis_index("tm")
    bands = [lax.dynamic_slice_in_dim(padded, me * block_cols, width, 2)]
    marks = [lax.dynamic_slice_in_dim(flags, me * window_cols, window_cols, 1)]
    for k in range(1, time_devices):
        route = [((i + k) % time_devices, i) for i in range(time_devices)]
        target = (me + time_devices - k) % time_devices
        block = lax.dynamic_slice_in_dim(padded, target * block_cols, width, 2)
        mark = lax.dynamic_slice_in_dim(flags, target * window_cols, window_cols, 1)
        bands.append(lax.ppermute(block, "tm", route))
        marks.append(lax.ppermute(mark, "tm", route))
    own = jnp.concatenate(bands, axis=0)
    marks = jnp.concatenate(marks, axis=0)
    marks = jnp.pad(marks, ((0, 0), (0, LANES - window_cols)))
    pieces = [own]
    for shift in range(1, WIN // band_rows):
        route = [(i + shift, i) for i in range(space_devices - shift)]
        pieces.append(lax.ppermute(own, "space", route))
    layout = [[(p, f) for p in range(len(pieces))] for f in range(own.shape[0])]
    return correlate(lags, marks, layout, pieces, window_cols)


def solution(mesh):
    return jax.shard_map(
        per_device,
        mesh=mesh,
        in_specs=(P("tm", "space", None), P("tm", "space", None), P()),
        out_specs=P("space", "tm", None, None),
        check_vma=False,
    )
```

```python
import functools
import math

import jax
import jax.numpy as jnp
import numpy as np
from jax import lax
from jax.experimental import pallas as pl
from jax.experimental.pallas import tpu as pltpu
from jax.sharding import PartitionSpec as P

WIN = 64
STRIDE = 16
SPAN = 32
HALF = WIN // 2
GROUP = 8
LANES = 128
BLOCK = GROUP * STRIDE
REACH = 2 * BLOCK
EXTRA = WIN - STRIDE
PARTS = 1


def split_table(table):
    table = np.asarray(table, np.float32)
    high = jnp.asarray(table).astype(jnp.bfloat16)
    low = (jnp.asarray(table) - high.astype(jnp.float32)).astype(jnp.bfloat16)
    return high, low


def turn(product):
    return 2.0 * math.pi / WIN * np.asarray(np.mod(product, WIN), np.float64)


def forward_rows():
    place = np.arange(WIN)
    u = np.arange(HALF)
    cos_rows = np.cos(turn(np.outer(u, place)))
    sin_rows = -np.sin(turn(np.outer(u, place)))
    sin_rows[0] = np.cos(turn(HALF * place))
    return np.concatenate([cos_rows, sin_rows], axis=0)


def forward_cols():
    rows = forward_rows()
    table = np.zeros((REACH, 2, GROUP, HALF))
    for g in range(GROUP):
        table[g * STRIDE : g * STRIDE + WIN, 0, g] = rows[:HALF].T
        table[g * STRIDE : g * STRIDE + WIN, 1, g] = rows[HALF:].T
    return table.reshape(REACH, 2 * GROUP * HALF)


def inverse_parts():
    place = np.arange(SPAN) - SPAN // 2
    u = np.arange(HALF)
    cos_part = np.cos(turn(np.outer(place, u)))
    sin_part = np.sin(turn(np.outer(place, u)))
    sin_part[:, 0] = np.cos(turn(HALF * place))
    return cos_part, sin_part


def inverse_rows(lag_count):
    cos_part, sin_part = inverse_parts()
    sin_part = -sin_part
    sin_part[:, 0] = -sin_part[:, 0]
    both = np.concatenate([cos_part, sin_part], axis=1)
    table = both.reshape(SPAN // 8, 2, 4, 1, 1, 2 * HALF).transpose(0, 2, 1, 3, 4, 5)
    table = np.broadcast_to(table, (SPAN // 8, 4, 2, lag_count, lag_count, 2 * HALF))
    return table.reshape(SPAN * lag_count, lag_count * 2 * HALF)


def inverse_cols():
    cos_part, sin_part = inverse_parts()
    table = np.zeros((2, GROUP, HALF, GROUP, SPAN))
    for g in range(GROUP):
        table[0, g, :, g] = cos_part.T
        table[1, g, :, g] = sin_part.T
    scale = 2.0 / (WIN * WIN * WIN)
    return table.reshape(2 * GROUP * HALF, GROUP * SPAN) * scale


def halves(value):
    high = value.astype(jnp.bfloat16)
    low = (value - high.astype(jnp.float32)).astype(jnp.bfloat16)
    return high, low


def mul(a, b):
    return jnp.dot(a, b, preferred_element_type=jnp.float32)


def cross_direct(ps, qs, lag_count):
    frame_count = len(ps)
    results = []
    for lag in range(1, lag_count + 1):
        real = imag = None
        for f in range(frame_count):
            g = (f + lag) % frame_count
            re = ps[f] * ps[g] + qs[f] * qs[g]
            im = ps[f] * qs[g] - qs[f] * ps[g]
            real = re if real is None else real + re
            imag = im if imag is None else imag + im
        results.append((real * frame_count, imag * frame_count))
    return results


def cross_eight(ps, qs):
    root = math.sqrt(0.5)
    sr = [ps[t] + ps[t + 4] for t in range(4)]
    si = [qs[t] + qs[t + 4] for t in range(4)]
    dr = [ps[t] - ps[t + 4] for t in range(4)]
    di = [qs[t] - qs[t + 4] for t in range(4)]
    e0r, e0i, e1r, e1i = sr[0] + sr[2], si[0] + si[2], sr[0] - sr[2], si[0] - si[2]
    o0r, o0i, o1r, o1i = sr[1] + sr[3], si[1] + si[3], sr[1] - sr[3], si[1] - si[3]

    def power(re, im):
        return re * re + im * im

    p0 = power(e0r + o0r, e0i + o0i)
    p4 = power(e0r - o0r, e0i - o0i)
    p2 = power(e1r + o1i, e1i - o1r)
    p6 = power(e1r - o1i, e1i + o1r)
    gpr, gpi, gmr, gmi = dr[0] + di[2], di[0] - dr[2], dr[0] - di[2], di[0] + dr[2]
    ar, ai, br, bi = dr[1] - dr[3], di[1] - di[3], dr[1] + dr[3], di[1] + di[3]
    hpr, hpi = root * (ar + bi), root * (ai - br)
    hmr, hmi = root * (bi - ar), root * (br + ai)
    p1 = power(gpr + hpr, gpi + hpi)
    p5 = power(gpr - hpr, gpi - hpi)
    p3 = power(gmr + hmr, gmi - hmi)
    p7 = power(gmr - hmr, gmi + hmi)
    a, b, c, d = p0 + p4, p0 - p4, p2 + p6, p2 - p6
    e, f, g, h = p1 + p5, p1 - p5, p3 + p7, p3 - p7
    less, more = root * (f - h), root * (f + h)
    return [
        (b + less, d + more),
        (a - c, e - g),
        (b - less, more - d),
        ((a + c) - (e + g), None),
    ]


def kernel(
    layout, frame_count, lag_count, block_count,
    lags_ref, *rest,
):
    stored, rest = rest[:7], rest[7:]
    piece_count = len(rest) - 22
    pieces, result_ref = rest[:piece_count], rest[piece_count]
    out_ref, *held = rest[piece_count + 12 : piece_count + 20]
    table_sems, out_sems = rest[piece_count + 20 :]
    loads = [
        pltpu.make_async_copy(a, b, table_sems.at[n]) for n, (a, b) in enumerate(zip(stored, held))
    ]
    for load in loads:
        load.start()
    ty_ref, txh_ref, txl_ref, iyh_ref, iyl_ref, ixh_ref, ixl_ref = held
    stores = []
    high_ref, low_ref, energy_ref, spec_ref, gain_ref, y_ref = rest[piece_count + 1 : piece_count + 7]
    part_ref, final_ref, pickh_ref, pickl_ref, tyuse_ref = rest[piece_count + 7 : piece_count + 12]
    wide = GROUP * HALF
    rows_per = 2 * HALF
    width = pieces[0].shape[-1]

    lane = lax.broadcasted_iota(jnp.int32, (8, LANES), 1)
    sub = lax.broadcasted_iota(jnp.int32, (8, LANES), 0)
    m0 = lane % HALF == 0
    r0 = sub == 0
    co = jnp.logical_and(m0, r0)
    first_half = lane < LANES // 2
    even = (lane // SPAN) % 2 == 0
    slot0 = lax.broadcasted_iota(jnp.int32, (frame_count, wide), 1) % HALF == 0

    column = lax.broadcasted_iota(jnp.int32, (REACH, wide), 0)
    owner = lax.broadcasted_iota(jnp.int32, (REACH, wide), 1) // HALF
    inside = jnp.logical_and(column >= owner * STRIDE, column < owner * STRIDE + WIN)
    band = inside.astype(jnp.float32).astype(jnp.bfloat16)
    same = (column // HALF == owner).astype(jnp.float32).astype(jnp.bfloat16)

    odd = lax.axis_index("space") % 2 == 1
    loads[0].wait()
    ty = jnp.where(odd, ty_ref[1].astype(jnp.float32), ty_ref[0].astype(jnp.float32))
    tyuse_ref[...] = ty.astype(jnp.bfloat16)

    wide_row0 = lax.broadcasted_iota(jnp.int32, (8, width), 0) == 0
    tail = slice(width - LANES, width)
    marks = jnp.concatenate(
        [pieces[layout[f][0][0]][layout[f][0][1], :1, tail] for f in range(frame_count)], axis=0
    ).astype(jnp.bfloat16)
    for f in range(frame_count):
        image = jnp.concatenate([pieces[p][q] for p, q in layout[f]], axis=0)
        high, low = halves(image)
        middle = mul(tyuse_ref[...], jnp.concatenate([high, low, high], axis=0))
        high, low = halves(middle)
        high_ref[f * rows_per : (f + 1) * rows_per, :] = high
        low_ref[f * rows_per : (f + 1) * rows_per, :] = low
        total = None
        for t in range(rows_per // 8):
            value = middle[8 * t : 8 * t + 8]
            square = value * value
            if t == 0:
                square = jnp.where(wide_row0, 0.0, square)
            if t == HALF // 8:
                square = jnp.where(wide_row0, 0.5 * square, square)
            total = square if total is None else total + square
        energy_ref[f : f + 1, :] = jnp.sum(total, axis=0, keepdims=True)

    for load in loads[1:]:
        load.wait()
    chosen = lax.broadcasted_iota(jnp.int32, iyh_ref.shape, 0) % lag_count
    wanted = jnp.zeros(iyh_ref.shape, jnp.int32)
    for k in range(lag_count):
        wanted = jnp.where(chosen == k, lags_ref[k], wanted)
    block_of = lax.broadcasted_iota(jnp.int32, iyh_ref.shape, 1) // rows_per + 1
    keep = wanted == block_of
    pickh_ref[...] = jnp.where(keep, iyh_ref[...].astype(jnp.float32), 0.0).astype(jnp.bfloat16)
    pickl_ref[...] = jnp.where(keep, iyl_ref[...].astype(jnp.float32), 0.0).astype(jnp.bfloat16)

    scales = {}

    def forward_unit(i, n, part, parts):
        columns = slice(i * BLOCK, i * BLOCK + REACH)
        count = frame_count * rows_per // parts
        rows = slice(part * count, (part + 1) * count)
        at = slice(n * wide, (n + 1) * wide)
        spec_ref[i, rows, at] = (
            mul(high_ref[rows, columns], txh_ref[:, at])
            + mul(low_ref[rows, columns], txh_ref[:, at])
            + mul(high_ref[rows, columns], txl_ref[:, at])
        )

    def gain_unit(i):
        columns = slice(i * BLOCK, i * BLOCK + REACH)
        zero = jnp.concatenate(
            [spec_ref[i, f * rows_per : f * rows_per + 1, :] for f in range(frame_count)], axis=0
        )
        zero_re, zero_im = zero[:, :wide], zero[:, wide:]
        line = jnp.where(slot0, 0.5 * zero_im * zero_im, zero_re * zero_re + zero_im * zero_im)
        high, low = halves(line)
        line = mul(high, same) + mul(low, same)
        high, low = halves(energy_ref[:, columns])
        rest_of = mul(high, band) + mul(low, band)
        variance = rest_of * (2.0 * WIN / WIN**4) + line * (2.0 / WIN**4)

        flag_row = lax.broadcasted_iota(jnp.int32, (LANES, wide), 0)
        flag_lane = lax.broadcasted_iota(jnp.int32, (LANES, wide), 1)
        first = EXTRA + (lax.axis_index("tm") * block_count + i) * GROUP
        pick = (flag_row == first + flag_lane // HALF).astype(jnp.float32).astype(jnp.bfloat16)
        flags = mul(marks, pick)
        gain_ref[i] = flags / jnp.sqrt(variance + 1e-06)

        counts = []
        for number in range(lag_count):
            ahead = jnp.concatenate([flags[number + 1 :], flags[: number + 1]], axis=0)
            counts.append(jnp.sum(flags * ahead, axis=0, keepdims=True))
        scale_rows = []
        for k in range(lag_count):
            count = counts[0]
            for number in range(1, lag_count):
                count = jnp.where(lags_ref[k] == number + 1, counts[number], count)
            scale_rows.append(1.0 / jnp.maximum(count, 1.0))
        scales[i] = jnp.concatenate(scale_rows * (8 // lag_count), axis=0)

    if frame_count == 8 and lag_count == 4:
        cross = cross_eight
    else:
        cross = functools.partial(cross_direct, lag_count=lag_count)

    def cross_unit(i, l, t):
        at = slice(l * LANES, (l + 1) * LANES)
        at_im = slice(wide + l * LANES, wide + (l + 1) * LANES)
        p0s, q0s, p1s, q1s, ends = [], [], [], [], []
        for f in range(frame_count):
            gain = jnp.broadcast_to(gain_ref[i, f : f + 1, at], (8, LANES))
            upper = slice(f * rows_per + 8 * t, f * rows_per + 8 * t + 8)
            lower = slice(f * rows_per + HALF + 8 * t, f * rows_per + HALF + 8 * t + 8)
            a = spec_ref[i, upper, at] * gain
            b = spec_ref[i, upper, at_im] * gain
            c = spec_ref[i, lower, at] * gain
            d = spec_ref[i, lower, at_im] * gain
            p0 = a - jnp.where(m0, 0.0, d)
            q0 = c + jnp.where(m0, 0.0, b)
            p1 = jnp.where(m0, b, a + d)
            q1 = jnp.where(m0, d, c - b)
            if t == 0:
                p0 = jnp.where(co, 0.0, jnp.where(r0, a, p0))
                q0 = jnp.where(r0, b, q0)
                p1 = jnp.where(r0, c, p1)
                q1 = jnp.where(co, 0.0, jnp.where(r0, d, q1))
                ends.append(jnp.where(co, d, 0.0))
            p0s.append(p0)
            q0s.append(q0)
            p1s.append(p1)
            q1s.append(q1)
        results0 = cross(p0s, q0s)
        results1 = cross(p1s, q1s)
        for number in range(lag_count):
            p0, q0 = results0[number]
            p1, q1 = results1[number]
            if q0 is None:
                ya = jnp.where(m0, p0, p0 + p1)
                yb = jnp.where(m0, p1, 0.0)
                yc = jnp.zeros_like(p0)
                yd = jnp.where(m0, 0.0, p0 - p1)
                q0 = q1 = yc
            else:
                ya = jnp.where(m0, p0, p0 + p1)
                yb = jnp.where(m0, p1, q1 - q0)
                yc = jnp.where(m0, q0, q0 + q1)
                yd = jnp.where(m0, q1, p0 - p1)
            if t == 0:
                last = ends[0] * ends[number + 1]
                for f in range(1, frame_count):
                    last = last + ends[f] * ends[(f + number + 1) % frame_count]
                ya = jnp.where(co, 0.0, jnp.where(r0, p0, ya))
                yb = jnp.where(co, 0.5 * p0, jnp.where(r0, -q0, yb))
                yc = jnp.where(co, 0.5 * p1, jnp.where(r0, p1, yc))
                yd = jnp.where(co, (0.5 * frame_count) * last, jnp.where(r0, -q1, yd))
            top = slice(number * rows_per + 8 * t, number * rows_per + 8 * t + 8)
            bottom = slice(number * rows_per + HALF + 8 * t, number * rows_per + HALF + 8 * t + 8)
            y_ref[i, top, at] = ya
            y_ref[i, top, at_im] = yb
            y_ref[i, bottom, at] = yc
            y_ref[i, bottom, at_im] = yd

    def inverse_unit(i, step):
        if step < 2:
            at = slice(step * wide, (step + 1) * wide)
            high, low = halves(y_ref[i, :, at])
            part_ref[i, :, at] = (
                mul(pickh_ref[...], high) + mul(pickh_ref[...], low) + mul(pickl_ref[...], high)
            )
        elif step == 2:
            high, low = halves(part_ref[i])
            final_ref[i] = mul(high, ixh_ref[...]) + mul(low, ixh_ref[...]) + mul(high, ixl_ref[...])
        else:
            scale = scales[i]
            for run in range(SPAN // 8):
                for l in range(GROUP * SPAN // LANES):
                    at = slice(l * LANES, (l + 1) * LANES)
                    v = []
                    for j in range(4):
                        r = (run * 4 + j) * 8
                        v.append(final_ref[i, r : r + 8, at] * scale[:, at])
                    for j in range(2):
                        x, y = v[j], v[j + 2]
                        v[j] = jnp.where(first_half, x, pltpu.roll(y, LANES // 2, 1))
                        v[j + 2] = jnp.where(first_half, pltpu.roll(x, LANES // 2, 1), y)
                    for j in (0, 2):
                        x, y = v[j], v[j + 1]
                        v[j] = jnp.where(even, x, pltpu.roll(y, SPAN, 1))
                        v[j + 1] = jnp.where(even, pltpu.roll(x, LANES - SPAN, 1), y)
                    for j in range(4):
                        window = i * GROUP + 4 * l + j
                        for side in range(2):
                            first = (2 * run + side) * LANES
                            out_ref[window, :, first : first + LANES] = v[j][4 * side : 4 * side + 4]
            done = pl.ds(i * GROUP, GROUP)
            store = pltpu.make_async_copy(out_ref.at[done], result_ref.at[0, done], out_sems.at[i])
            store.start()
            stores.append(store)

    spots = [(l, t) for l in range(wide // LANES) for t in range(HALF // 8)]
    for n in range(2):
        for part in range(PARTS):
            forward_unit(0, n, part, PARTS)
    gain_unit(0)
    for i in range(block_count + 1):
        queue = []
        if i > 0:
            queue += [functools.partial(inverse_unit, i - 1, step) for step in range(4)]
        if i + 1 < block_count:
            ahead = [
                functools.partial(forward_unit, i + 1, n, part, PARTS)
                for n in range(2)
                for part in range(PARTS)
            ]
            merged = []
            while queue or ahead:
                merged += ahead[:1] + queue[:1]
                queue, ahead = queue[1:], ahead[1:]
            queue = merged + [functools.partial(gain_unit, i + 1)]
        if i < block_count:
            for number, (l, t) in enumerate(spots):
                take = len(queue) * (number + 1) // len(spots) - len(queue) * number // len(spots)
                done = len(queue) * number // len(spots)
                for unit in queue[done : done + take]:
                    unit()
                cross_unit(i, l, t)
        else:
            for unit in queue:
                unit()
    for store in stores:
        store.wait()


def correlate(lags, layout, pieces, window_cols):
    frame_count = len(layout)
    lag_count = lags.shape[0]
    wide = GROUP * HALF
    width = pieces[0].shape[-1]
    block_count = window_cols // GROUP
    rows = forward_rows()
    quarter = rows.reshape(2 * HALF, WIN // STRIDE, STRIDE)
    choices = []
    for order in ((0, 1, 2, 3), (0, 3, 2, 1)):
        ty_high, ty_low = split_table(quarter[:, order, :].reshape(rows.shape))
        choices.append(jnp.concatenate([ty_high, ty_high, ty_low], axis=1))
    ty = jnp.stack(choices)
    txh, txl = split_table(forward_cols())
    iyh, iyl = split_table(inverse_rows(lag_count))
    ixh, ixl = split_table(inverse_cols() / frame_count)
    vmem = pl.BlockSpec(memory_space=pltpu.VMEM)
    hbm = pl.BlockSpec(memory_space=pl.ANY)
    tables = (ty, txh, txl, iyh, iyl, ixh, ixl)
    body = functools.partial(kernel, layout, frame_count, lag_count, block_count)
    return pl.pallas_call(
        body,
        out_shape=jax.ShapeDtypeStruct((1, window_cols, lag_count, SPAN * SPAN), jnp.float32),
        in_specs=[pl.BlockSpec(memory_space=pltpu.SMEM)] + [hbm] * 7 + [vmem] * len(pieces),
        out_specs=hbm,
        scratch_shapes=[
            pltpu.VMEM((frame_count * 2 * HALF, width), jnp.bfloat16),
            pltpu.VMEM((frame_count * 2 * HALF, width), jnp.bfloat16),
            pltpu.VMEM((frame_count, width), jnp.float32),
            pltpu.VMEM((block_count, frame_count * 2 * HALF, 2 * wide), jnp.float32),
            pltpu.VMEM((block_count, frame_count, wide), jnp.float32),
            pltpu.VMEM((block_count, lag_count * 2 * HALF, 2 * wide), jnp.float32),
            pltpu.VMEM((block_count, lag_count * SPAN, 2 * wide), jnp.float32),
            pltpu.VMEM((block_count, lag_count * SPAN, GROUP * SPAN), jnp.float32),
            pltpu.VMEM(iyh.shape, jnp.bfloat16),
            pltpu.VMEM(iyl.shape, jnp.bfloat16),
            pltpu.VMEM(ty.shape[1:], jnp.bfloat16),
            pltpu.VMEM((window_cols, lag_count, SPAN * SPAN), jnp.float32),
            *[pltpu.VMEM(table.shape, table.dtype) for table in tables],
            pltpu.SemaphoreType.DMA((len(tables),)),
            pltpu.SemaphoreType.DMA((block_count,)),
        ],
    )(lags, ty, txh, txl, iyh, iyl, ixh, ixl, *[pltpu.with_memory_space_constraint(x, pltpu.VMEM) for x in pieces])


def shifted(block, devices, source):
    time_devices, space_devices = devices
    route = []
    for a in range(time_devices):
        for s in range(space_devices):
            b, r = source(a, s)
            if r < space_devices:
                route.append((b % time_devices * space_devices + r, a * space_devices + s))
    return lax.ppermute(block, ("tm", "space"), route)


def per_device(frames, seeding, lags):
    frame_count, band_rows, columns = frames.shape
    time_devices = lax.axis_size("tm")
    space_devices = lax.axis_size("space")
    devices = (time_devices, space_devices)
    block_cols = columns // time_devices
    window_cols = block_cols // STRIDE
    width = block_cols + LANES
    me = lax.axis_index("tm")
    padded = jnp.pad(frames, ((0, 0), (0, 0), (0, width)))
    room = LANES - EXTRA - seeding.shape[2]
    marks = jnp.pad(seeding.astype(jnp.float32), ((0, 0), (0, 0), (block_cols + EXTRA, room)))
    place = lax.broadcasted_iota(jnp.int32, (1, 1, width), 2)

    def block_for(target):
        block = lax.dynamic_slice_in_dim(padded, target * block_cols, width, 2)
        return jnp.where(place < block_cols + EXTRA, block, marks)

    starts, far, near, again = [], [], [], []
    for k in range(time_devices):
        block = block_for((me + time_devices - k) % time_devices)
        far.append(shifted(block, devices, lambda a, s: (a + k, s + 2)))
        near.append(shifted(block, devices, lambda a, s: (a + k, s + 3 if s % 2 else s + 1)))
        starts.append(block if k == 0 else shifted(block, devices, lambda a, s: (a + k, s)))
    for k in range(time_devices):
        again.append(shifted(far[k], devices, lambda a, s: (a, s ^ 1)))
    pieces = starts + near + far + again
    layout = []
    for f in range(time_devices * frame_count):
        k, q = f // frame_count, f % frame_count
        layout.append([(k + group * time_devices, q) for group in range(4)])
    return correlate(lags, layout, pieces, window_cols)


def solution(mesh):
    return jax.shard_map(
        per_device,
        mesh=mesh,
        in_specs=(P("tm", "space", None), P("tm", "space", None), P()),
        out_specs=P("space", "tm", None, None),
        check_vma=False,
    )
```

```python
import functools
import math

import jax
import jax.numpy as jnp
import numpy as np
from jax import lax
from jax.experimental import pallas as pl
from jax.experimental.pallas import tpu as pltpu
from jax.sharding import PartitionSpec as P

WIN = 64
STRIDE = 16
SPAN = 32
HALF = WIN // 2
GROUP = 4
LANES = 128
BLOCK = GROUP * STRIDE
REACH = 2 * BLOCK
LOOK = 4
EXTRA = WIN - STRIDE
PARTS = 1


def split_table(table):
    table = np.asarray(table, np.float32)
    high = jnp.asarray(table).astype(jnp.bfloat16)
    low = (jnp.asarray(table) - high.astype(jnp.float32)).astype(jnp.bfloat16)
    return high, low


def turn(product):
    return 2.0 * math.pi / WIN * np.asarray(np.mod(product, WIN), np.float64)


def forward_rows():
    place = np.arange(WIN)
    u = np.arange(HALF)
    cos_rows = np.cos(turn(np.outer(u, place)))
    sin_rows = -np.sin(turn(np.outer(u, place)))
    sin_rows[0] = np.cos(turn(HALF * place))
    return np.concatenate([cos_rows, sin_rows], axis=0)


def forward_cols():
    rows = forward_rows()
    table = np.zeros((REACH, 2, GROUP, HALF))
    for g in range(GROUP):
        table[g * STRIDE : g * STRIDE + WIN, 0, g] = rows[:HALF].T
        table[g * STRIDE : g * STRIDE + WIN, 1, g] = rows[HALF:].T
    return table.reshape(REACH, 2 * GROUP * HALF)


def inverse_parts():
    place = np.arange(SPAN) - SPAN // 2
    u = np.arange(HALF)
    cos_part = np.cos(turn(np.outer(place, u)))
    sin_part = np.sin(turn(np.outer(place, u)))
    sin_part[:, 0] = np.cos(turn(HALF * place))
    return cos_part, sin_part


def inverse_rows(lag_count):
    cos_part, sin_part = inverse_parts()
    sin_part = -sin_part
    sin_part[:, 0] = -sin_part[:, 0]
    both = np.concatenate([cos_part, sin_part], axis=1)
    table = both.reshape(SPAN // 8, 2, 4, 1, 1, 2 * HALF).transpose(0, 2, 1, 3, 4, 5)
    table = np.broadcast_to(table, (SPAN // 8, 4, 2, lag_count, lag_count, 2 * HALF))
    return table.reshape(SPAN * lag_count, lag_count * 2 * HALF)


def inverse_cols():
    cos_part, sin_part = inverse_parts()
    table = np.zeros((2, GROUP, HALF, GROUP, SPAN))
    for g in range(GROUP):
        table[0, g, :, g] = cos_part.T
        table[1, g, :, g] = sin_part.T
    scale = 2.0 / (WIN * WIN * WIN)
    return table.reshape(2 * GROUP * HALF, GROUP * SPAN) * scale


def halves(value):
    high = value.astype(jnp.bfloat16)
    low = (value - high.astype(jnp.float32)).astype(jnp.bfloat16)
    return high, low


def mul(a, b):
    return jnp.dot(a, b, preferred_element_type=jnp.float32)


def cross_direct(ps, qs, lag_count):
    frame_count = len(ps)
    results = []
    for lag in range(1, lag_count + 1):
        real = imag = None
        for f in range(frame_count):
            g = (f + lag) % frame_count
            re = ps[f] * ps[g] + qs[f] * qs[g]
            im = ps[f] * qs[g] - qs[f] * ps[g]
            real = re if real is None else real + re
            imag = im if imag is None else imag + im
        results.append((real * frame_count, imag * frame_count))
    return results


def cross_eight(ps, qs):
    root = math.sqrt(0.5)
    sr = [ps[t] + ps[t + 4] for t in range(4)]
    si = [qs[t] + qs[t + 4] for t in range(4)]
    dr = [ps[t] - ps[t + 4] for t in range(4)]
    di = [qs[t] - qs[t + 4] for t in range(4)]
    e0r, e0i, e1r, e1i = sr[0] + sr[2], si[0] + si[2], sr[0] - sr[2], si[0] - si[2]
    o0r, o0i, o1r, o1i = sr[1] + sr[3], si[1] + si[3], sr[1] - sr[3], si[1] - si[3]

    def power(re, im):
        return re * re + im * im

    p0 = power(e0r + o0r, e0i + o0i)
    p4 = power(e0r - o0r, e0i - o0i)
    p2 = power(e1r + o1i, e1i - o1r)
    p6 = power(e1r - o1i, e1i + o1r)
    gpr, gpi, gmr, gmi = dr[0] + di[2], di[0] - dr[2], dr[0] - di[2], di[0] + dr[2]
    ar, ai, br, bi = dr[1] - dr[3], di[1] - di[3], dr[1] + dr[3], di[1] + di[3]
    hpr, hpi = root * (ar + bi), root * (ai - br)
    hmr, hmi = root * (bi - ar), root * (br + ai)
    p1 = power(gpr + hpr, gpi + hpi)
    p5 = power(gpr - hpr, gpi - hpi)
    p3 = power(gmr + hmr, gmi - hmi)
    p7 = power(gmr - hmr, gmi + hmi)
    a, b, c, d = p0 + p4, p0 - p4, p2 + p6, p2 - p6
    e, f, g, h = p1 + p5, p1 - p5, p3 + p7, p3 - p7
    less, more = root * (f - h), root * (f + h)
    return [
        (b + less, d + more),
        (a - c, e - g),
        (b - less, more - d),
        ((a + c) - (e + g), None),
    ]


def vertical(image, ty, high_ref, low_ref, energy_ref, place):
    rows_per = 2 * HALF
    rows = slice(place * rows_per, (place + 1) * rows_per)
    row0 = lax.broadcasted_iota(jnp.int32, (8, image.shape[1]), 0) == 0
    high, low = halves(image)
    middle = mul(ty, jnp.concatenate([high, low, high], axis=0))
    high, low = halves(middle)
    high_ref[rows, :] = high
    low_ref[rows, :] = low
    total = None
    for t in range(rows_per // 8):
        value = middle[8 * t : 8 * t + 8]
        square = value * value
        if t == 0:
            square = jnp.where(row0, 0.0, square)
        if t == HALF // 8:
            square = jnp.where(row0, 0.5 * square, square)
        total = square if total is None else total + square
    energy_ref[place : place + 1, :] = jnp.sum(total, axis=0, keepdims=True)


def forward(m, rows, high_ref, low_ref, spec_ref, txk_ref, txh_ref, txl_ref):
    at = slice(m // 2 * REACH, (m // 2 + 1 + m % 2) * REACH)
    high, low = high_ref[rows, at], low_ref[rows, at]
    if m % 2 == 0:
        both = jnp.concatenate([high, low], axis=1)
        spec_ref[m, rows, :] = mul(both, txk_ref[...]) + mul(high, txl_ref[:REACH])
    else:
        spec_ref[m, rows, :] = (
            mul(high, txh_ref[...]) + mul(low, txh_ref[...]) + mul(high, txl_ref[REACH:])
        )


def first_kernel(
    layout, lag_count, block_count,
    lags_ref, tys_at, txk_at, txh_at, txl_at, iyh_at, iyl_at, ixh_at, ixl_at, *rest,
):
    pieces, rest = rest[: len(layout[0])], rest[len(layout[0]) :]
    ty_ref, txk_ref, txh_ref, txl_ref, pickh_ref, pickl_ref, ixh_ref, ixl_ref = rest[:8]
    spec_ref, energy_ref, tys_ref, iyh_ref, iyl_ref, high_ref, low_ref, sems = rest[8:]
    frame_count = len(layout)
    rows_per = 2 * HALF
    moves = (
        (tys_at, tys_ref), (txk_at, txk_ref), (txh_at, txh_ref), (txl_at, txl_ref),
        (iyh_at, iyh_ref), (iyl_at, iyl_ref), (ixh_at, ixh_ref), (ixl_at, ixl_ref),
    )
    loads = [pltpu.make_async_copy(a, b, sems.at[n]) for n, (a, b) in enumerate(moves)]
    for load in loads:
        load.start()
    odd = lax.axis_index("space") % 2 == 1
    loads[0].wait()
    ty = jnp.where(odd, tys_ref[1].astype(jnp.float32), tys_ref[0].astype(jnp.float32))
    ty_ref[...] = ty.astype(jnp.bfloat16)
    for f in range(frame_count):
        image = jnp.concatenate([pieces[p][q] for p, q in layout[f]], axis=0)
        vertical(image, ty_ref[...], high_ref, low_ref, energy_ref, f)
    for load in loads[1:]:
        load.wait()
    for m in range(block_count):
        forward(m, slice(0, frame_count * rows_per), high_ref, low_ref, spec_ref, txk_ref, txh_ref, txl_ref)
    chosen = lax.broadcasted_iota(jnp.int32, iyh_ref.shape, 0) % lag_count
    wanted = jnp.zeros(iyh_ref.shape, jnp.int32)
    for k in range(lag_count):
        wanted = jnp.where(chosen == k, lags_ref[k], wanted)
    block_of = lax.broadcasted_iota(jnp.int32, iyh_ref.shape, 1) // rows_per + 1
    keep = wanted == block_of
    pickh_ref[...] = jnp.where(keep, iyh_ref[...].astype(jnp.float32), 0.0).astype(jnp.bfloat16)
    pickl_ref[...] = jnp.where(keep, iyl_ref[...].astype(jnp.float32), 0.0).astype(jnp.bfloat16)


def second_kernel(layout, own_count, lag_count, block_count, lags_ref, *rest):
    ty_ref, txk_ref, txh_ref, txl_ref, pickh_ref, pickl_ref, ixh_ref, ixl_ref = rest[:8]
    own_spec_ref, own_energy_ref, own_piece, rest = rest[8], rest[9], rest[10], rest[11:]
    pieces, rest = rest[:-13], rest[-13:]
    result_ref, high_ref, low_ref, late_energy_ref, energy_ref, moved_ref, late_spec_ref = rest[:7]
    gain_ref, y_ref, part_ref, final_ref, out_ref, out_sems = rest[7:]
    late_count = len(layout)
    frame_count = own_count + late_count
    wide = GROUP * HALF
    rows_per = 2 * HALF
    width = own_piece.shape[-1]
    stores = []

    lane = lax.broadcasted_iota(jnp.int32, (8, LANES), 1)
    sub = lax.broadcasted_iota(jnp.int32, (8, LANES), 0)
    m0 = lane % HALF == 0
    r0 = sub == 0
    co = jnp.logical_and(m0, r0)
    first_half = lane < LANES // 2
    even = (lane // SPAN) % 2 == 0
    slot0 = lax.broadcasted_iota(jnp.int32, (frame_count, wide), 1) % HALF == 0

    column = lax.broadcasted_iota(jnp.int32, (REACH, wide), 0)
    owner = lax.broadcasted_iota(jnp.int32, (REACH, wide), 1) // HALF
    inside = jnp.logical_and(column >= owner * STRIDE, column < owner * STRIDE + WIN)
    band = inside.astype(jnp.float32).astype(jnp.bfloat16)
    same = (column // HALF == owner).astype(jnp.float32).astype(jnp.bfloat16)

    tail = slice(width - LANES, width)
    marks = [own_piece[f, :1, tail] for f in range(own_count)]
    marks += [pieces[layout[f][0][0]][layout[f][0][1], :1, tail] for f in range(late_count)]
    marks = jnp.concatenate(marks, axis=0).astype(jnp.bfloat16)
    scales = {}

    def spectrum(m, f, begin, stop):
        if f < own_count:
            return own_spec_ref[m, f * rows_per + begin : f * rows_per + stop, :]
        g = f - own_count
        return late_spec_ref[m, g * rows_per + begin : g * rows_per + stop, :]

    def forward_unit(m, part, parts):
        count = late_count * rows_per // parts
        rows = slice(part * count, (part + 1) * count)
        forward(m, rows, high_ref, low_ref, late_spec_ref, txk_ref, txh_ref, txl_ref)

    def twice(value, table):
        high, low = halves(value)
        result = mul(jnp.concatenate([high, low], axis=0), table)
        return result[:frame_count] + result[frame_count:]

    def gain_unit(m):
        zero = jnp.concatenate(
            [spectrum(m, f, 0, 1) for f in range(frame_count)], axis=0
        )
        zero_re, zero_im = zero[:, :wide], zero[:, wide:]
        line = jnp.where(slot0, 0.5 * zero_im * zero_im, zero_re * zero_re + zero_im * zero_im)
        source = (energy_ref, moved_ref)[m % 2]
        energy = source[:, m // 2 * REACH : m // 2 * REACH + REACH]
        variance = twice(energy, band) * (2.0 * WIN / WIN**4) + twice(line, same) * (2.0 / WIN**4)

        flag_row = lax.broadcasted_iota(jnp.int32, (LANES, wide), 0)
        flag_lane = lax.broadcasted_iota(jnp.int32, (LANES, wide), 1)
        first = EXTRA + (lax.axis_index("tm") * block_count + m) * GROUP
        pick = (flag_row == first + flag_lane // HALF).astype(jnp.float32).astype(jnp.bfloat16)
        flags = mul(marks, pick)
        gain_ref[m] = flags / jnp.sqrt(variance + 1e-06)

        counts = []
        for number in range(lag_count):
            ahead = jnp.concatenate([flags[number + 1 :], flags[: number + 1]], axis=0)
            counts.append(jnp.sum(flags * ahead, axis=0, keepdims=True))
        scale_rows = []
        for k in range(lag_count):
            count = counts[0]
            for number in range(1, lag_count):
                count = jnp.where(lags_ref[k] == number + 1, counts[number], count)
            scale_rows.append(1.0 / jnp.maximum(count, 1.0))
        scales[m] = jnp.concatenate(scale_rows * (8 // lag_count), axis=0)

    if frame_count == 8 and lag_count == 4:
        cross = cross_eight
    else:
        cross = functools.partial(cross_direct, lag_count=lag_count)

    def cross_unit(i, t):
        at = slice(0, LANES)
        at_im = slice(LANES, 2 * LANES)
        p0s, q0s, p1s, q1s, ends = [], [], [], [], []
        for f in range(frame_count):
            gain = jnp.broadcast_to(gain_ref[i, f : f + 1, at], (8, LANES))
            upper = spectrum(i, f, 8 * t, 8 * t + 8)
            lower = spectrum(i, f, HALF + 8 * t, HALF + 8 * t + 8)
            a, b = upper[:, at] * gain, upper[:, at_im] * gain
            c, d = lower[:, at] * gain, lower[:, at_im] * gain
            p0 = a - jnp.where(m0, 0.0, d)
            q0 = c + jnp.where(m0, 0.0, b)
            p1 = jnp.where(m0, b, a + d)
            q1 = jnp.where(m0, d, c - b)
            if t == 0:
                p0 = jnp.where(co, 0.0, jnp.where(r0, a, p0))
                q0 = jnp.where(r0, b, q0)
                p1 = jnp.where(r0, c, p1)
                q1 = jnp.where(co, 0.0, jnp.where(r0, d, q1))
                ends.append(jnp.where(co, d, 0.0))
            p0s.append(p0)
            q0s.append(q0)
            p1s.append(p1)
            q1s.append(q1)
        results0 = cross(p0s, q0s)
        results1 = cross(p1s, q1s)
        for number in range(lag_count):
            p0, q0 = results0[number]
            p1, q1 = results1[number]
            if q0 is None:
                ya = jnp.where(m0, p0, p0 + p1)
                yb = jnp.where(m0, p1, 0.0)
                yc = jnp.zeros_like(p0)
                yd = jnp.where(m0, 0.0, p0 - p1)
                q0 = q1 = yc
            else:
                ya = jnp.where(m0, p0, p0 + p1)
                yb = jnp.where(m0, p1, q1 - q0)
                yc = jnp.where(m0, q0, q0 + q1)
                yd = jnp.where(m0, q1, p0 - p1)
            if t == 0:
                last = ends[0] * ends[number + 1]
                for f in range(1, frame_count):
                    last = last + ends[f] * ends[(f + number + 1) % frame_count]
                ya = jnp.where(co, 0.0, jnp.where(r0, p0, ya))
                yb = jnp.where(co, 0.5 * p0, jnp.where(r0, -q0, yb))
                yc = jnp.where(co, 0.5 * p1, jnp.where(r0, p1, yc))
                yd = jnp.where(co, (0.5 * frame_count) * last, jnp.where(r0, -q1, yd))
            top = slice(number * rows_per + 8 * t, number * rows_per + 8 * t + 8)
            bottom = slice(number * rows_per + HALF + 8 * t, number * rows_per + HALF + 8 * t + 8)
            y_ref[i, top, at] = ya
            y_ref[i, top, at_im] = yb
            y_ref[i, bottom, at] = yc
            y_ref[i, bottom, at_im] = yd

    def inverse_unit(i, step):
        if step == 0:
            high, low = halves(y_ref[i])
            part_ref[i] = (
                mul(pickh_ref[...], high) + mul(pickh_ref[...], low) + mul(pickl_ref[...], high)
            )
        elif step == 1:
            high, low = halves(part_ref[i])
            final_ref[i] = mul(high, ixh_ref[...]) + mul(low, ixh_ref[...]) + mul(high, ixl_ref[...])
        else:
            scale = scales[i]
            for run in range(SPAN // 8):
                v = []
                for j in range(4):
                    r = (run * 4 + j) * 8
                    v.append(final_ref[i, r : r + 8, :] * scale)
                for j in range(2):
                    x, y = v[j], v[j + 2]
                    v[j] = jnp.where(first_half, x, pltpu.roll(y, LANES // 2, 1))
                    v[j + 2] = jnp.where(first_half, pltpu.roll(x, LANES // 2, 1), y)
                for j in (0, 2):
                    x, y = v[j], v[j + 1]
                    v[j] = jnp.where(even, x, pltpu.roll(y, SPAN, 1))
                    v[j + 1] = jnp.where(even, pltpu.roll(x, LANES - SPAN, 1), y)
                for j in range(4):
                    for side in range(2):
                        first = (2 * run + side) * LANES
                        out_ref[i * GROUP + j, :, first : first + LANES] = v[j][4 * side : 4 * side + 4]
            done = pl.ds(i * GROUP, GROUP)
            store = pltpu.make_async_copy(out_ref.at[done], result_ref.at[0, done], out_sems.at[i])
            store.start()
            stores.append(store)

    bind = functools.partial
    early = range(min(LOOK, block_count))
    for f in range(late_count):
        image = jnp.concatenate([pieces[p][q] for p, q in layout[f]], axis=0)
        vertical(image, ty_ref[...], high_ref, low_ref, late_energy_ref, f)
    for m in early:
        forward_unit(m, 0, 1)
    energy_ref[...] = jnp.concatenate([own_energy_ref[...], late_energy_ref[...]], axis=0)
    moved_ref[...] = pltpu.roll(energy_ref[...], width - BLOCK, 1)
    gain_unit(0)
    spots = HALF // 8
    for i in range(block_count + 1):
        queue = []
        if 0 < i:
            queue += [bind(inverse_unit, i - 1, step) for step in range(3)]
        if i + LOOK < block_count:
            queue.insert(0, bind(forward_unit, i + LOOK, 0, 1))
        if i + 1 < block_count:
            queue.insert(min(1, len(queue)), bind(gain_unit, i + 1))
        if i < block_count:
            for t in range(spots):
                begin, end = len(queue) * t // spots, len(queue) * (t + 1) // spots
                for unit in queue[begin:end]:
                    unit()
                cross_unit(i, t)
        else:
            for unit in queue:
                unit()
    for store in stores:
        store.wait()


def correlate(lags, layout, pieces, window_cols, own_count):
    frame_count = len(layout)
    lag_count = lags.shape[0]
    wide = GROUP * HALF
    width = pieces[0].shape[-1]
    block_count = window_cols // GROUP
    rows = forward_rows()
    quarter = rows.reshape(2 * HALF, WIN // STRIDE, STRIDE)
    choices = []
    for order in ((0, 1, 2, 3), (0, 3, 2, 1)):
        ty_high, ty_low = split_table(quarter[:, order, :].reshape(rows.shape))
        choices.append(jnp.concatenate([ty_high, ty_high, ty_low], axis=1))
    ty = jnp.stack(choices)
    txh, txl = split_table(forward_cols())
    late = np.zeros((2 * REACH, 2 * wide), np.float32)
    late[BLOCK : BLOCK + REACH] = forward_cols()
    txk = jnp.concatenate([txh, txh], axis=0)
    lateh, latel = split_table(late)
    txl = jnp.concatenate([txl, latel], axis=0)
    iyh, iyl = split_table(inverse_rows(lag_count))
    ixh, ixl = split_table(inverse_cols() / frame_count)
    vmem = pl.BlockSpec(memory_space=pltpu.VMEM)
    hbm = pl.BlockSpec(memory_space=pl.ANY)
    smem = pl.BlockSpec(memory_space=pltpu.SMEM)
    tables = (ty, txk, lateh, txl, iyh, iyl, ixh, ixl)
    narrow = jnp.bfloat16
    full = 2 * HALF

    def gathered(part):
        names = sorted({p for spots in part for p, _ in spots})
        new_layout = [[(names.index(p), q) for p, q in spots] for spots in part]
        return [pltpu.with_memory_space_constraint(pieces[p], pltpu.VMEM) for p in names], new_layout

    def fixed(value):
        return pltpu.with_memory_space_constraint(value, pltpu.HBM)

    own_pieces, own_layout = gathered(layout[:own_count])
    late_pieces, late_layout = gathered(layout[own_count:])
    late_count = frame_count - own_count
    with jax.named_scope("early"):
        kept = pl.pallas_call(
            functools.partial(first_kernel, own_layout, lag_count, block_count),
            out_shape=[
                pltpu.VMEM(ty.shape[1:], narrow),
                *[pltpu.VMEM(table.shape, narrow) for table in tables[1:]],
                pltpu.VMEM((block_count, own_count * full, 2 * wide), jnp.float32),
                pltpu.VMEM((own_count, width), jnp.float32),
            ],
            in_specs=[smem] + [hbm] * len(tables) + [vmem] * len(own_pieces),
            out_specs=[vmem] * 10,
            scratch_shapes=[
                pltpu.VMEM(ty.shape, narrow),
                pltpu.VMEM(iyh.shape, narrow),
                pltpu.VMEM(iyl.shape, narrow),
                pltpu.VMEM((own_count * full, width), narrow),
                pltpu.VMEM((own_count * full, width), narrow),
                pltpu.SemaphoreType.DMA((len(tables),)),
            ],
            compiler_params=pltpu.CompilerParams(vmem_limit_bytes=16 << 20),
        )(fixed(lags), *[fixed(table) for table in tables], *own_pieces)
    own_piece = pltpu.with_memory_space_constraint(pieces[layout[0][0][0]], pltpu.VMEM)
    return pl.pallas_call(
        functools.partial(second_kernel, late_layout, own_count, lag_count, block_count),
        out_shape=jax.ShapeDtypeStruct((1, window_cols, lag_count, SPAN * SPAN), jnp.float32),
        in_specs=[smem] + [vmem] * (11 + len(late_pieces)),
        out_specs=hbm,
        scratch_shapes=[
            pltpu.VMEM((late_count * full, width), narrow),
            pltpu.VMEM((late_count * full, width), narrow),
            pltpu.VMEM((late_count, width), jnp.float32),
            pltpu.VMEM((frame_count, width), jnp.float32),
            pltpu.VMEM((frame_count, width), jnp.float32),
            pltpu.VMEM((block_count, late_count * full, 2 * wide), jnp.float32),
            pltpu.VMEM((block_count, frame_count, wide), jnp.float32),
            pltpu.VMEM((block_count, lag_count * full, 2 * wide), jnp.float32),
            pltpu.VMEM((block_count, lag_count * SPAN, 2 * wide), jnp.float32),
            pltpu.VMEM((block_count, lag_count * SPAN, GROUP * SPAN), jnp.float32),
            pltpu.VMEM((window_cols, lag_count, SPAN * SPAN), jnp.float32),
            pltpu.SemaphoreType.DMA((block_count,)),
        ],
        compiler_params=pltpu.CompilerParams(vmem_limit_bytes=24 << 20),
    )(fixed(lags), *[pltpu.with_memory_space_constraint(x, pltpu.VMEM) for x in kept], own_piece, *late_pieces)


def shifted(block, devices, source):
    time_devices, space_devices = devices
    route = []
    for a in range(time_devices):
        for s in range(space_devices):
            b, r = source(a, s)
            if r < space_devices:
                route.append((b % time_devices * space_devices + r, a * space_devices + s))
    return lax.ppermute(block, ("tm", "space"), route)


def per_device(frames, seeding, lags):
    frame_count, band_rows, columns = frames.shape
    time_devices = lax.axis_size("tm")
    space_devices = lax.axis_size("space")
    devices = (time_devices, space_devices)
    block_cols = columns // time_devices
    window_cols = block_cols // STRIDE
    width = block_cols + LANES
    me = lax.axis_index("tm")
    padded = jnp.pad(frames, ((0, 0), (0, 0), (0, width)))
    room = LANES - EXTRA - seeding.shape[2]
    marks = jnp.pad(seeding.astype(jnp.float32), ((0, 0), (0, 0), (block_cols + EXTRA, room)))
    place = lax.broadcasted_iota(jnp.int32, (1, 1, width), 2)

    def block_for(target):
        block = lax.dynamic_slice_in_dim(padded, target * block_cols, width, 2)
        return jnp.where(place < block_cols + EXTRA, block, marks)

    starts, far, near, again = [], [], [], []
    for k in range(time_devices):
        block = block_for((me + time_devices - k) % time_devices)
        far.append(shifted(block, devices, lambda a, s: (a + k, s + 2)))
        near.append(shifted(block, devices, lambda a, s: (a + k, s + 3 if s % 2 else s + 1)))
        starts.append(block if k == 0 else shifted(block, devices, lambda a, s: (a + k, s)))
    for k in range(time_devices):
        again.append(shifted(far[k], devices, lambda a, s: (a, s ^ 1)))
    pieces = starts + near + far + again
    layout = []
    for f in range(time_devices * frame_count):
        k, q = f // frame_count, f % frame_count
        layout.append([(k + group * time_devices, q) for group in range(4)])
    return correlate(lags, layout, pieces, window_cols, frame_count)


def solution(mesh):
    return jax.shard_map(
        per_device,
        mesh=mesh,
        in_specs=(P("tm", "space", None), P("tm", "space", None), P()),
        out_specs=P("space", "tm", None, None),
        check_vma=False,
    )
```
